32 devices in a mesh: tiles: 2 (over x), date: 8 (over z, y), row: 2 (over core).
Axes of the slice: x: 2, y: 2, z: 4, core: 2. Of those that a mesh axis runs over, the one named last changes fastest.
Arguments:
- slc_stack: bfloat16 [16, 2, 256, 1024], P('date', None, ('tiles', 'row')), parts along dimension 2, as said below
- partners: int32 [16, 4], P('date'), may hold values from 0 to 15, as said below
- counts: int32 [16], P('date'), may hold values from 1 to 4, as said below
- windows: int32 [16, 4], P('date'), may hold values from 3 to 5
Outputs:
- coherence: bfloat16 [16, 4, 256, 1024], P('date', None, ('tiles', 'row')), parts along dimension 2
The draws below stay inside these ranges and needn't reach their ends.
There are 2 independent parts, one for each index of `tiles`. The reference program is written for one: setup_inputs(seed, part) draws one part's arguments, and reference() takes and returns one part's arrays. A program takes and returns all parts, laid end to end along the dimension named above; an argument that names none is the same for every part. Nothing has to cross between parts.
Inputs may be any that keep to these rules, and one draw needn't show every extreme that they name: The partners of date d are (d + o) mod 16 for distinct offsets o from 1 to 4; some date has a first partner exactly 4 ahead. `counts`: of the 2 dates held by one device along `date`, at most one has more than 2 pairs, so those dates have 6 pairs or fewer together; some device's pair of dates has exactly 6, and some date has 4. `slc_stack`: every pixel's magnitude is 0.5 or more.
All inputs are finite; a program needn't handle non-finite values.
Results may differ from the reference program's by a relative error of at most 0.001.
Values may be sent and summed in bfloat16 or wider, within the bound.
No kernel may reach another device: no remote copies, remote signals or barrier semaphores. Data moves between devices by JAX's collectives and lax.ppermute only.
A program may use at most 64 MiB of HBM per device.

```python
import math
import jax
import jax.numpy as jnp
from jax import lax

DATES_DEV = 2
COLS = 1024
MAXOFF = 4
MAXP = 4
HALF = 2
NDATES = 16
ROWS = 128


def draw_slc_stack(key, part):
    keys = jax.random.split(key, 4)
    base_phase = jax.random.uniform(keys[0], (1, ROWS, COLS), jnp.float32, -math.pi, math.pi)
    spread = jnp.exp(jax.random.uniform(keys[1], (NDATES, 1, 1), jnp.float32, math.log(0.2), math.log(2.5)))
    amplitude = jnp.exp(jax.random.uniform(keys[2], (NDATES, ROWS, COLS), jnp.float32, math.log(0.5), math.log(4.0)))
    noise = jax.random.normal(keys[3], (NDATES, ROWS, COLS), jnp.float32)
    phase = base_phase + spread * noise
    real_part = amplitude * jnp.cos(phase)
    imag_part = amplitude * jnp.sin(phase)
    return jnp.stack([real_part, imag_part], axis=1).astype(jnp.bfloat16)


def draw_partners(key, part):
    scores = jax.random.randint(key, (NDATES, MAXOFF), 0, 1 << 20) * MAXOFF + jnp.arange(MAXOFF, dtype=jnp.int32)[None, :]
    offsets = jnp.argsort(scores, axis=1, stable=True).astype(jnp.int32) + 1
    far_place = jnp.argmax(offsets == MAXOFF, axis=1).astype(jnp.int32)
    column_ids = jnp.arange(MAXOFF, dtype=jnp.int32)[None, :]
    swapped = jnp.where(column_ids == 0, MAXOFF, jnp.where(column_ids == far_place[:, None], offsets[:, 0:1], offsets))
    date_ids = jnp.arange(NDATES, dtype=jnp.int32)[:, None]
    forced = jnp.logical_or(date_ids == NDATES - MAXOFF, date_ids == NDATES - 1 - MAXOFF)
    offsets = jnp.where(forced, swapped, offsets)
    return ((date_ids + offsets[:, 0:MAXP]) % NDATES).astype(jnp.int32)


def draw_counts(key, part):
    groups = NDATES // DATES_DEV
    keys = [jax.random.fold_in(key, 21 + number) for number in range(4)]
    base_counts = jax.random.randint(keys[0], (groups, DATES_DEV), 1, HALF + 1)
    heavy_place = jax.random.randint(keys[1], (groups, 1), 0, DATES_DEV)
    heavy_count = jax.random.randint(keys[2], (groups, 1), 1, MAXP + 1)
    column_ids = jnp.arange(DATES_DEV, dtype=jnp.int32)[None, :]
    result = jnp.where(column_ids == heavy_place, heavy_count, base_counts)
    full_group = jax.random.randint(keys[3], (), 0, groups)
    forced = jnp.where(column_ids == heavy_place, MAXP, HALF)
    group_ids = jnp.arange(groups, dtype=jnp.int32)[:, None]
    result = jnp.where(group_ids == full_group, forced, result)
    return result.reshape(NDATES).astype(jnp.int32)


def place_ends(entries, own_key, low, largest):
    index_at = [jax.random.randint(jax.random.fold_in(own_key, axis), (), 0, length) for axis, length in enumerate(entries.shape)]
    main_axis = entries.shape.index(max(entries.shape))
    neighbour = index_at[:main_axis] + [(index_at[main_axis] + 1) % entries.shape[main_axis]] + index_at[main_axis + 1:]
    return entries.at[tuple(index_at)].set(low).at[tuple(neighbour)].set(largest)


def setup_inputs(seed: int = 0, part: int = 0) -> dict:
    seeds = jax.random.split(jax.random.key(seed), 5)
    part_keys = jax.random.split(jax.random.fold_in(seeds[4], part), 5)
    return {
        "slc_stack": draw_slc_stack(jax.random.fold_in(jax.random.fold_in(seeds[4], part), 71), part),
        "partners": draw_partners(jax.random.fold_in(seeds[4], 71), part),
        "counts": draw_counts(jax.random.fold_in(seeds[4], 71), part),
        "windows": place_ends(jax.random.randint(seeds[3], (NDATES, MAXP), 3, 6), jax.random.fold_in(seeds[3], 1), 3, 5).astype(jnp.int32),
    }


def pair_products(first_block, second_block):
    first_re = first_block[0].astype(jnp.float32)
    first_im = first_block[1].astype(jnp.float32)
    second_re = second_block[0].astype(jnp.float32)
    second_im = second_block[1].astype(jnp.float32)
    cross_re = first_re * second_re + first_im * second_im
    cross_im = first_im * second_re - first_re * second_im
    power_first = first_re * first_re + first_im * first_im
    power_second = second_re * second_re + second_im * second_im
    return jnp.stack([cross_re, cross_im, power_first, power_second])

def range_boxcar(stacked, half_width):
    columns = stacked.shape[-1]
    padded = jnp.pad(stacked, ((0, 0), (0, 0), (5, 5)))
    summed = jnp.zeros_like(stacked)
    for offset in range(-5, 6):
        weight = jnp.where(half_width >= abs(offset), 1.0, 0.0).astype(jnp.float32)
        summed = summed + weight * padded[:, :, 5 + offset:5 + offset + columns]
    return summed

def row_boxcar(extended, strip_rows):
    summed = extended[:, 0:strip_rows, :]
    for offset in range(1, 5):
        summed = summed + extended[:, offset:offset + strip_rows, :]
    return summed

def coherence_of(sums):
    magnitude = jnp.sqrt(sums[0] * sums[0] + sums[1] * sums[1])
    return magnitude / jnp.sqrt(sums[2] * sums[3])

def reference(slc_stack, partners, counts, windows):
    total_dates = slc_stack.shape[0]
    per_date = partners.shape[1]
    slot_total = total_dates * per_date

    def one_pair(slot_id):
        own_date = slot_id // per_date
        slot_index = slot_id % per_date
        partner_date = partners[own_date, slot_index]
        half_width = windows[own_date, slot_index]
        stacked = pair_products(slc_stack[own_date], slc_stack[partner_date])
        summed = range_boxcar(stacked, half_width)
        padded = jnp.pad(summed, ((0, 0), (2, 2), (0, 0)))
        sums = row_boxcar(padded, summed.shape[1])
        result = coherence_of(sums)
        return jnp.where(slot_index < counts[own_date], result, 0.0).astype(jnp.bfloat16)
    blocks = lax.map(one_pair, jnp.arange(slot_total, dtype=jnp.int32))
    return blocks.reshape(total_dates, per_date, slc_stack.shape[2], slc_stack.shape[3])
```

```python
import functools

import jax
import jax.numpy as jnp
from jax import lax
from jax.experimental import pallas as pl
from jax.experimental.pallas import tpu as pltpu
from jax.sharding import PartitionSpec as P

REACH_COLS = 5
HALO = 2
LANES = 128
TOP = 8
SMALLEST = 1.1754944e-38


def stage_kernel(
    first_local,
    fill,
    total_dates,
    partners,
    counts,
    windows,
    own,
    own_edge,
    other,
    other_edge,
    previous,
    out,
    products,
    split,
    band,
    results,
    zeros,
    sems,
):
    del previous
    dates_dev, _, rows, cols = own.shape
    here = other.shape[0]
    per_date = partners.shape[1]
    slots = dates_dev * per_date
    stripes = cols // LANES
    first_date = lax.axis_index("date") * dates_dev
    upper = lax.axis_index("row") == 0

    def state(slot):
        date, place = slot // per_date, slot % per_date
        ahead = lax.rem(partners[date, place] - first_date + total_dates, total_dates) - first_local
        used = place < counts[date]
        mine = jnp.logical_and(used, jnp.logical_and(ahead >= 0, ahead < here))
        return date, place, jnp.clip(ahead, 0, here - 1), used, mine

    def copy_of(slot, source):
        return pltpu.make_async_copy(source, out.at[slot // per_date, slot % per_date], sems.at[slot])

    split[:, 0:LANES] = jnp.zeros((split.shape[0], LANES), jnp.bfloat16)
    split[:, LANES + cols :] = jnp.zeros((split.shape[0], LANES), jnp.bfloat16)
    if fill:
        zeros[...] = jnp.zeros_like(zeros)

        def clear(slot, carry):
            _, _, _, used, _ = state(slot)

            @pl.when(jnp.logical_not(used))
            def _():
                copy_of(slot, zeros).start()

            return carry

        lax.fori_loop(0, slots, clear, 0)

    def planes(first_re, first_im, second_re, second_im):
        first_re, first_im = first_re.astype(jnp.float32), first_im.astype(jnp.float32)
        second_re, second_im = second_re.astype(jnp.float32), second_im.astype(jnp.float32)
        return (
            first_re * second_re + first_im * second_im,
            first_im * second_re - first_re * second_im,
            first_re * first_re + first_im * first_im,
            second_re * second_re + second_im * second_im,
        )

    def one_slot(slot, carry):
        date, place, ahead, _, mine = state(slot)

        @pl.when(mine)
        def _():
            half_width = windows[date, place]
            depth = lax.broadcasted_iota(jnp.int32, band.shape, 0)
            width = lax.broadcasted_iota(jnp.int32, band.shape, 1)
            band[...] = jnp.where(jnp.abs(depth - LANES - width) <= half_width, 1.0, 0.0).astype(jnp.bfloat16)
            for stripe in range(stripes):
                at = slice(stripe * LANES, (stripe + 1) * LANES)
                main = planes(own[date, 0, :, at], own[date, 1, :, at], other[ahead, 0, :, at], other[ahead, 1, :, at])
                edge = planes(
                    own_edge[date, 0, :, at], own_edge[date, 1, :, at], other_edge[ahead, 0, :, at], other_edge[ahead, 1, :, at]
                )
                for k in range(4):
                    products[k, TOP : TOP + rows, :] = main[k]
                    products[k, TOP - HALO : TOP, :] = jnp.where(upper, 0.0, edge[k])
                    products[k, TOP + rows : TOP + rows + HALO, :] = jnp.where(upper, edge[k], 0.0)
                for k in range(4):
                    total = products[k, TOP - HALO : TOP - HALO + rows, :]
                    for shift in range(1, 2 * HALO + 1):
                        total = total + products[k, TOP - HALO + shift : TOP - HALO + shift + rows, :]
                    high = total.astype(jnp.bfloat16)
                    low = (total - high.astype(jnp.float32)).astype(jnp.bfloat16)
                    into = slice(LANES + stripe * LANES, LANES + (stripe + 1) * LANES)
                    split[k * 2 * rows : k * 2 * rows + rows, into] = high
                    split[k * 2 * rows + rows : (k + 1) * 2 * rows, into] = low
            block = band.shape[1]
            for j in range(cols // block):
                box = jnp.dot(
                    split[:, j * block : j * block + band.shape[0]], band[...], preferred_element_type=jnp.float32
                )
                sums = [box[k * 2 * rows : k * 2 * rows + rows] + box[k * 2 * rows + rows : (k + 1) * 2 * rows] for k in range(4)]
                square = sums[0] * sums[0] + sums[1] * sums[1]
                magnitude = square * lax.rsqrt(jnp.maximum(square, SMALLEST))
                value = magnitude * lax.rsqrt(sums[2] * sums[3])
                results[slot, :, j * block : (j + 1) * block] = value.astype(jnp.bfloat16)
            copy_of(slot, results.at[slot]).start()

        return carry

    lax.fori_loop(0, slots, one_slot, 0)

    def finish(slot, carry):
        _, _, _, used, mine = state(slot)
        started = jnp.logical_or(mine, jnp.logical_not(used)) if fill else mine

        @pl.when(started)
        def _():
            copy_of(slot, results.at[slot]).wait()

        return carry

    lax.fori_loop(0, slots, finish, 0)


def stage(first_local, total_dates, tables, own, own_edge, other, other_edge, previous):
    dates_dev, _, rows, cols = own.shape
    per_date = tables[0].shape[1]
    slots = dates_dev * per_date
    shape = jax.ShapeDtypeStruct((dates_dev, per_date, rows, cols), jnp.bfloat16)
    fill = previous is None
    kernel = functools.partial(stage_kernel, first_local, fill, total_dates)
    if fill:
        inner = kernel

        def kernel(*refs):
            inner(*refs[:7], None, *refs[7:])

    smem = pl.BlockSpec(memory_space=pltpu.SMEM)
    vmem = pl.BlockSpec(memory_space=pltpu.VMEM)
    anywhere = pl.BlockSpec(memory_space=pl.ANY)
    block = 2 * LANES
    return pl.pallas_call(
        kernel,
        out_shape=shape,
        in_specs=[smem] * 3 + [vmem] * 4 + ([] if fill else [anywhere]),
        out_specs=anywhere,
        scratch_shapes=[
            pltpu.VMEM((4, rows + 2 * TOP, LANES), jnp.float32),
            pltpu.VMEM((8 * rows, cols + 2 * LANES), jnp.bfloat16),
            pltpu.VMEM((2 * block, block), jnp.bfloat16),
            pltpu.VMEM((slots, rows, cols), jnp.bfloat16),
            pltpu.VMEM((rows, cols), jnp.bfloat16),
            pltpu.SemaphoreType.DMA((slots,)),
        ],
        input_output_aliases={} if fill else {7: 0},
        name=f"stage_{first_local}",
        cost_estimate=pl.CostEstimate(flops=1 << 30, bytes_accessed=1 << 22, transcendentals=0),
    )(*tables, own, own_edge, other, other_edge, *([] if fill else [previous]))


def local(slc_stack, partners, counts, windows):
    dates_dev, _, rows, _ = slc_stack.shape
    loop_size = lax.axis_size("date")
    strips = lax.axis_size("row")
    assert strips == 2
    reach = loop_size // 4
    total_dates = dates_dev * loop_size
    tables = (partners, counts, windows)
    edge = jnp.where(lax.axis_index("row") == 0, slc_stack[:, :, rows - HALO :], slc_stack[:, :, :HALO])
    blocks = []
    for distance in range(1, reach + 1):
        blocks.append(lax.ppermute(slc_stack, "date", [((i + distance) % loop_size, i) for i in range(loop_size)]))
    edges = []
    for distance in range(reach + 1):
        pairs = [
            (((i + distance) % loop_size) * strips + (1 - r), i * strips + r) for i in range(loop_size) for r in range(strips)
        ]
        edges.append(lax.ppermute(edge, ("date", "row"), pairs))
    out = stage(0, total_dates, tables, slc_stack, edges[0], slc_stack, edges[0], None)
    for distance in range(1, reach + 1):
        out = stage(
            distance * dates_dev, total_dates, tables, slc_stack, edges[0], blocks[distance - 1], edges[distance], out
        )
    return out


def solution(mesh):
    in_specs = (
        P("date", None, ("tiles", "row"), None),
        P("date", None),
        P("date"),
        P("date", None),
    )
    out_specs = P("date", None, ("tiles", "row"), None)
    return jax.shard_map(local, mesh=mesh, in_specs=in_specs, out_specs=out_specs, check_vma=False)
```

```python
import functools

import jax
import jax.numpy as jnp
from jax import lax
from jax.experimental import pallas as pl
from jax.experimental.pallas import tpu as pltpu
from jax.sharding import PartitionSpec as P


HALO = 2
LANES = 128
TOP = 8
SMALLEST = 1.1754944e-38


def stage_kernel(
    first_local,
    edge_start,
    fill,
    ahead_of,
    windows,
    own,
    own_edge,
    other,
    other_edge,
    previous,
    out,
    products,
    split,
    band,
    results,
    zeros,
    sems,
):
    del previous
    dates_dev, _, rows, cols = own.shape
    here = other.shape[0]
    per_date = windows.shape[1]
    slots = dates_dev * per_date
    stripes = cols // LANES
    upper = lax.axis_index("row") == 0

    def state(slot):
        date, place = slot // per_date, slot % per_date
        ahead = ahead_of[date, place]
        mine = jnp.logical_and(ahead >= first_local, ahead < first_local + here)
        return date, place, ahead, mine

    def copy_of(slot, source):
        return pltpu.make_async_copy(source, out.at[slot // per_date, slot % per_date], sems.at[slot])

    split[:, 0:LANES] = jnp.zeros((split.shape[0], LANES), jnp.bfloat16)
    split[:, LANES + cols :] = jnp.zeros((split.shape[0], LANES), jnp.bfloat16)
    if fill:
        zeros[...] = jnp.zeros_like(zeros)

        def clear(slot, carry):
            _, _, ahead, _ = state(slot)

            @pl.when(ahead < 0)
            def _():
                copy_of(slot, zeros).start()

            return carry

        lax.fori_loop(0, slots, clear, 0)

    def planes(first_re, first_im, second_re, second_im):
        first_re, first_im = first_re.astype(jnp.float32), first_im.astype(jnp.float32)
        second_re, second_im = second_re.astype(jnp.float32), second_im.astype(jnp.float32)
        return (
            first_re * second_re + first_im * second_im,
            first_im * second_re - first_re * second_im,
            first_re * first_re + first_im * first_im,
            second_re * second_re + second_im * second_im,
        )

    def one_slot(slot, carry):
        date, place, ahead, mine = state(slot)

        @pl.when(mine)
        def _():
            there = ahead - first_local
            half_width = windows[date, place]
            depth = lax.broadcasted_iota(jnp.int32, band.shape, 0)
            width = lax.broadcasted_iota(jnp.int32, band.shape, 1)
            band[...] = jnp.where(jnp.abs(depth - LANES - width) <= half_width, 1.0, 0.0).astype(jnp.bfloat16)
            for stripe in range(stripes):
                at = slice(stripe * LANES, (stripe + 1) * LANES)
                main = planes(own[date, 0, :, at], own[date, 1, :, at], other[there, 0, :, at], other[there, 1, :, at])
                edge = planes(
                    own_edge[date, 0, :, at], own_edge[date, 1, :, at], other_edge[edge_start + there, 0, :, at], other_edge[edge_start + there, 1, :, at]
                )
                for k in range(4):
                    products[k, TOP : TOP + rows, :] = main[k]
                    products[k, TOP - HALO : TOP, :] = jnp.where(upper, 0.0, edge[k])
                    products[k, TOP + rows : TOP + rows + HALO, :] = jnp.where(upper, edge[k], 0.0)
                for k in range(4):
                    total = products[k, TOP - HALO : TOP - HALO + rows, :]
                    for shift in range(1, 2 * HALO + 1):
                        total = total + products[k, TOP - HALO + shift : TOP - HALO + shift + rows, :]
                    high = total.astype(jnp.bfloat16)
                    low = (total - high.astype(jnp.float32)).astype(jnp.bfloat16)
                    into = slice(LANES + stripe * LANES, LANES + (stripe + 1) * LANES)
                    split[k * 2 * rows : k * 2 * rows + rows, into] = high
                    split[k * 2 * rows + rows : (k + 1) * 2 * rows, into] = low
            block = band.shape[1]
            for j in range(cols // block):
                box = jnp.dot(
                    split[:, j * block : j * block + band.shape[0]], band[...], preferred_element_type=jnp.float32
                )
                sums = [box[k * 2 * rows : k * 2 * rows + rows] + box[k * 2 * rows + rows : (k + 1) * 2 * rows] for k in range(4)]
                square = sums[0] * sums[0] + sums[1] * sums[1]
                magnitude = square * lax.rsqrt(jnp.maximum(square, SMALLEST))
                value = magnitude * lax.rsqrt(sums[2] * sums[3])
                results[slot, :, j * block : (j + 1) * block] = value.astype(jnp.bfloat16)
            copy_of(slot, results.at[slot]).start()

        return carry

    lax.fori_loop(0, slots, one_slot, 0)

    def finish(slot, carry):
        _, _, ahead, mine = state(slot)
        started = jnp.logical_or(mine, ahead < 0) if fill else mine

        @pl.when(started)
        def _():
            copy_of(slot, results.at[slot]).wait()

        return carry

    lax.fori_loop(0, slots, finish, 0)


def stage(first_local, tables, own, own_edge, other, other_edge, edge_start, previous):
    dates_dev, _, rows, cols = own.shape
    per_date = tables[1].shape[1]
    slots = dates_dev * per_date
    shape = jax.ShapeDtypeStruct((dates_dev, per_date, rows, cols), jnp.bfloat16)
    fill = previous is None
    kernel = functools.partial(stage_kernel, first_local, edge_start, fill)
    if fill:
        inner = kernel

        def kernel(*refs):
            inner(*refs[:6], None, *refs[6:])

    smem = pl.BlockSpec(memory_space=pltpu.SMEM)
    vmem = pl.BlockSpec(memory_space=pltpu.VMEM)
    anywhere = pl.BlockSpec(memory_space=pl.ANY)
    block = 2 * LANES
    return pl.pallas_call(
        kernel,
        out_shape=shape,
        in_specs=[smem] * 2 + [vmem] * 4 + ([] if fill else [anywhere]),
        out_specs=anywhere,
        scratch_shapes=[
            pltpu.VMEM((4, rows + 2 * TOP, LANES), jnp.float32),
            pltpu.VMEM((8 * rows, cols + 2 * LANES), jnp.bfloat16),
            pltpu.VMEM((2 * block, block), jnp.bfloat16),
            pltpu.VMEM((slots, rows, cols), jnp.bfloat16),
            pltpu.VMEM((rows, cols), jnp.bfloat16),
            pltpu.SemaphoreType.DMA((slots,)),
        ],
        input_output_aliases={} if fill else {6: 0},
        compiler_params=pltpu.CompilerParams(vmem_limit_bytes=16 << 20),
        cost_estimate=pl.CostEstimate(flops=1 << 30, bytes_accessed=1 << 22, transcendentals=0),
    )(*tables, own, own_edge, other, other_edge, *([] if fill else [previous]))


def relayed(slc_stack, edges, loop_size):
    first, second = slc_stack[0:1], lax.optimization_barrier(slc_stack)[1:2]
    by_two = [((i + 2) % loop_size, i) for i in range(loop_size)]
    by_one = [((i + 1) % loop_size, i) for i in range(loop_size)]
    far_first = lax.ppermute(first, "date", by_two)
    near_second = lax.ppermute(second, "date", by_one)
    far_second = lax.ppermute(second, "date", by_two)
    near_direct = lax.ppermute(first, "date", [(i + 1, i) for i in range(0, loop_size, 2)])
    near_relayed = lax.ppermute(far_first, "date", [(i - 1, i) for i in range(1, loop_size, 2)])
    odd = lax.rem(lax.axis_index("date"), 2) == 1
    near_first = jnp.where(odd, near_relayed, near_direct)
    return [
        (4, far_first, edges[2], 0),
        (3, near_second, edges[1], 1),
        (2, near_first, edges[1], 0),
        (5, far_second, edges[2], 1),
    ]


def whole(slc_stack, partners, counts, windows):
    dates_dev, _, rows, _ = slc_stack.shape
    loop_size = lax.axis_size("date")
    strips = lax.axis_size("row")
    assert strips == 2
    reach = loop_size // 4
    total_dates = dates_dev * loop_size
    first_date = lax.axis_index("date") * dates_dev
    ahead_of = jnp.where(partners < first_date, partners + total_dates, partners) - first_date
    used = lax.broadcasted_iota(jnp.int32, partners.shape, 1) < counts[:, None]
    tables = (jnp.where(used, ahead_of, -1), windows)
    edge = jnp.where(lax.axis_index("row") == 0, slc_stack[:, :, rows - HALO :], slc_stack[:, :, :HALO])
    edges = []
    for distance in range(reach + 1):
        pairs = [
            (((i + distance) % loop_size) * strips + (1 - r), i * strips + r) for i in range(loop_size) for r in range(strips)
        ]
        edges.append(lax.ppermute(edge, ("date", "row"), pairs))
    out = stage(0, tables, slc_stack, edges[0], slc_stack, edges[0], 0, None)
    if reach == 2 and dates_dev == 2:
        arrivals = relayed(slc_stack, edges, loop_size)
    else:
        arrivals = []
        for distance in range(1, reach + 1):
            block = lax.ppermute(slc_stack, "date", [((i + distance) % loop_size, i) for i in range(loop_size)])
            arrivals.append((distance * dates_dev, block, edges[distance], 0))
    for first_local, block, block_edge, edge_start in arrivals:
        out = stage(first_local, tables, slc_stack, edges[0], block, block_edge, edge_start, out)
    return out


def solution(mesh):
    in_specs = (
        P("date", None, ("tiles", "row"), None),
        P("date", None),
        P("date"),
        P("date", None),
    )
    out_specs = P("date", None, ("tiles", "row"), None)
    return jax.shard_map(whole, mesh=mesh, in_specs=in_specs, out_specs=out_specs, check_vma=False)
```

```python
import functools

import jax
import jax.numpy as jnp
from jax import lax
from jax.experimental import pallas as pl
from jax.experimental.pallas import tpu as pltpu
from jax.sharding import PartitionSpec as P


NARROW = 3
WIDE = 5
HALO = 2
LANES = 128
BLOCK = 2 * LANES
TOP = 8
SMALLEST = 1.1754944e-38
CODE = 8


def band_table():
    shape = (WIDE - NARROW + 1, 2 * BLOCK, BLOCK)
    width = lax.broadcasted_iota(jnp.int32, shape, 0) + NARROW
    off = lax.broadcasted_iota(jnp.int32, shape, 1) - LANES - lax.broadcasted_iota(jnp.int32, shape, 2)
    return jnp.where(jnp.abs(off) <= width, 1.0, 0.0).astype(jnp.bfloat16)


def stage_kernel(role, rows_of, layout, span, places, final_rows, blocks, *refs):
    table, bands, own, own_edge, *refs = refs
    other, refs = refs[:blocks], refs[blocks:]
    dates_dev, _, rows, cols = own.shape
    here = len(rows_of)
    stripes = cols // LANES
    wide = BLOCK // LANES
    near_stripes = range(max(0, span[0] * wide - 1), min(stripes, span[1] * wide + 1))
    upper = lax.axis_index("row") == 0
    if role == "first":
        results, own_box, products, split, other_power = refs
    elif role == "middle":
        own_box, results, products, split, other_power = refs
    elif role == "gather":
        own_box, *refs = refs
        earlier, refs = refs[: len(places)], refs[len(places) :]
        out, products, split, other_power, results, sems, zeros, zero_sems = refs
    else:
        own_box, _, out, products, split, other_power, results, sems = refs
    codes = table[...]

    def pad(ref, at):
        if span[0] == 0:
            ref[at, :, 0:LANES] = jnp.zeros((ref.shape[1], LANES), jnp.bfloat16)
        if span[1] * BLOCK == cols:
            ref[at, :, LANES + cols :] = jnp.zeros((ref.shape[1], LANES), jnp.bfloat16)

    def over_rows(ref, at, stripe, k, main, edge):
        products[k, TOP : TOP + rows, :] = main
        products[k, TOP - HALO : TOP, :] = jnp.where(upper, 0.0, edge)
        products[k, TOP + rows : TOP + rows + HALO, :] = jnp.where(upper, edge, 0.0)
        total = products[k, TOP - HALO : TOP - HALO + rows, :]
        for shift in range(1, 2 * HALO + 1):
            total = total + products[k, TOP - HALO + shift : TOP - HALO + shift + rows, :]
        high = total.astype(jnp.bfloat16)
        low = (total - high.astype(jnp.float32)).astype(jnp.bfloat16)
        into = slice(LANES + stripe * LANES, LANES + (stripe + 1) * LANES)
        ref[at, 2 * k * rows : (2 * k + 1) * rows, into] = high
        ref[at, (2 * k + 1) * rows : (2 * k + 2) * rows, into] = low

    def stripe_of(ref, at, stripe):
        columns = slice(stripe * LANES, (stripe + 1) * LANES)
        return tuple(ref[at, plane, :, columns].astype(jnp.float32) for plane in range(2))

    def own_stripe(date, stripe):
        return *stripe_of(own, date, stripe), *stripe_of(own_edge, date, stripe)

    def other_stripe(t, stripe):
        if layout is None:
            return *stripe_of(other[0], t, stripe), *stripe_of(other[1], t, stripe)
        found = []
        for (k, start, base), size in zip(layout(stripe), (rows, rows, HALO, HALO)):
            if len(other[k].shape) == 4:
                found.append(other[k][start, base, :, stripe * LANES : (stripe + 1) * LANES].astype(jnp.float32))
                continue
            columns = slice((stripe - base) * LANES, (stripe - base + 1) * LANES)
            found.append(other[k][0, start : start + size, columns].astype(jnp.float32))
        return found

    def fill_power(ref, at, source, source_at):
        pad(ref, at)
        for stripe in near_stripes:
            re, im, edge_re, edge_im = source(source_at, stripe)
            over_rows(ref, at, stripe, 0, re * re + im * im, edge_re * edge_re + edge_im * edge_im)

    def over_columns(parts, width):
        box = jnp.dot(jnp.concatenate(parts, axis=0), bands[width], preferred_element_type=jnp.float32)
        return [box[k : k + rows] + box[k + rows : k + 2 * rows] for k in range(0, box.shape[0], 2 * rows)]

    def fill_box(power, date):
        for width in range(bands.shape[0]):
            for j in range(*span):
                (total,) = over_columns([power[date, :, j * BLOCK : (j + 2) * BLOCK]], width)
                own_box[date, width, :, j * BLOCK : (j + 1) * BLOCK] = total

    def pair(t, date, code):
        width = code % CODE - NARROW
        for stripe in near_stripes:
            u_re, u_im, ue_re, ue_im = own_stripe(date, stripe)
            v_re, v_im, ve_re, ve_im = other_stripe(t, stripe)
            over_rows(split, 0, stripe, 0, u_re * v_re + u_im * v_im, ue_re * ve_re + ue_im * ve_im)
            over_rows(split, 0, stripe, 1, u_im * v_re - u_re * v_im, ue_im * ve_re - ue_re * ve_im)
        for j in range(*span):
            at = slice(j * BLOCK, (j + 2) * BLOCK)
            re, im, power = over_columns([split[0, :, at], other_power[t, :, at]], width)
            square = re * re + im * im
            magnitude = square * lax.rsqrt(jnp.maximum(square, SMALLEST))
            value = magnitude * lax.rsqrt(own_box[date, width, :, j * BLOCK : (j + 1) * BLOCK] * power)
            results[t * dates_dev + date, :, j * BLOCK : (j + 1) * BLOCK] = value.astype(jnp.bfloat16)

    def copy_of(ref, at, date, slot, number):
        source, target = ref.at[at], out.at[date, slot]
        if ref is results and span != (0, cols // BLOCK):
            columns = slice(span[0] * BLOCK, span[1] * BLOCK)
            source, target = ref.at[at, :, columns], out.at[date, slot, :, columns]
        return pltpu.make_async_copy(source, target, sems.at[number + at])

    def copies_of(ref, rows_at, number):
        found = []
        for t, row in enumerate(rows_at):
            for date in range(dates_dev):
                code, at = codes[row, date], t * dates_dev + date
                found.append((code >= 0, copy_of(ref, at, date, jnp.maximum(code, 0) // CODE, number)))
        return found

    def zero_copies():
        found = []
        for date in range(dates_dev):
            held = [codes[row, date] // CODE for rows_at in (*places, rows_of, final_rows) for row in rows_at]
            for slot in range(out.shape[1]):
                empty = functools.reduce(jnp.logical_and, [code != slot for code in held])
                at = date * out.shape[1] + slot
                found.append((empty, pltpu.make_async_copy(zeros, out.at[date, slot], zero_sems.at[at])))
        return found

    def each(items, action):
        for condition, copy in items:

            @pl.when(condition)
            def _(copy=copy):
                getattr(copy, action)()

    pending, own_copies = [], []
    if role == "gather":
        zeros[...] = jnp.zeros_like(zeros)
        number = here * dates_dev
        for ref, rows_at in zip(earlier, places):
            pending += copies_of(ref, rows_at, number)
            number += len(rows_at) * dates_dev
        pending += zero_copies()
        each(pending, "start")
    if role in ("gather", "final"):
        own_copies = copies_of(results, rows_of, 0)
    if role == "first":
        for date in range(dates_dev):
            fill_power(other_power, date, own_stripe, date)
            fill_box(other_power, date)
    for t, row in enumerate(rows_of):
        found = [codes[row, date] for date in range(dates_dev)]

        @pl.when(functools.reduce(jnp.maximum, found) >= 0)
        def _(t=t, found=found):
            pad(split, 0)
            if role != "first":
                fill_power(other_power, t, other_stripe, t)

            def body(date, carry):
                code = found[0]
                for k in range(1, dates_dev):
                    code = jnp.where(date == k, found[k], code)

                @pl.when(code >= 0)
                def _():
                    pair(t, date, code)
                    if own_copies:
                        copy_of(results, t * dates_dev + date, date, code // CODE, 0).start()

                return carry

            lax.fori_loop(0, dates_dev, body, 0)

    each(pending + own_copies, "wait")


def stage(role, rows_of, tables, own, own_edge, other, layout, span, *state, places=(), final_rows=(), slots=None):
    dates_dev, _, rows, cols = own.shape
    here = len(rows_of)
    vmem, anywhere = pl.BlockSpec(memory_space=pltpu.VMEM), pl.BlockSpec(memory_space=pl.ANY)
    padded = cols + BLOCK
    span = span or (0, cols // BLOCK)
    results = (here * dates_dev, rows, cols)
    scratch = [pltpu.VMEM((2, rows + 2 * TOP, LANES), jnp.float32), pltpu.VMEM((1, 4 * rows, padded), jnp.bfloat16)]
    scratch.append(pltpu.VMEM((here, 2 * rows, padded), jnp.bfloat16))
    out_shape, out_specs = jax.ShapeDtypeStruct(results, jnp.bfloat16), vmem
    if role == "first":
        out_shape = (out_shape, jax.ShapeDtypeStruct((dates_dev, WIDE - NARROW + 1, rows, cols), jnp.float32))
        out_specs = (vmem, vmem)
    args = [*tables, own, own_edge, *other, *state]
    in_specs = [vmem] * len(args)
    aliases = {}
    if role in ("gather", "final"):
        out_shape, out_specs = jax.ShapeDtypeStruct((dates_dev, slots, rows, cols), jnp.bfloat16), anywhere
        count = here + sum(len(p) for p in places)
        scratch += [pltpu.VMEM(results, jnp.bfloat16), pltpu.SemaphoreType.DMA((count * dates_dev,))]
    if role == "gather":
        scratch += [pltpu.VMEM((rows, cols), jnp.bfloat16), pltpu.SemaphoreType.DMA((dates_dev * slots,))]
    if role == "final":
        in_specs[-1] = anywhere
        aliases = {len(args) - 1: 0}
    return pl.pallas_call(
        functools.partial(stage_kernel, role, rows_of, layout, span, places, final_rows, len(other)),
        out_shape=out_shape,
        in_specs=in_specs,
        out_specs=out_specs,
        scratch_shapes=scratch,
        input_output_aliases=aliases,
        compiler_params=pltpu.CompilerParams(vmem_limit_bytes=16 << 20),
        cost_estimate=pl.CostEstimate(flops=1 << 30, bytes_accessed=1 << 22, transcendentals=0),
    )(*args)


def gather_rows(part, own, pieces):
    rows = own.shape[2]
    for k, (date, plane, column) in enumerate(pieces):
        part[0, k * rows : (k + 1) * rows] = own[date, plane, :, column : column + part.shape[2]]


def prepare_kernel(pieces, own, edge, *parts):
    dates_dev, planes, rows, _ = own.shape
    upper = lax.axis_index("row") == 0
    for part, pieces_of in zip(parts, pieces):
        gather_rows(part, own, pieces_of)
    for date in range(dates_dev):
        for plane in range(planes):
            edge[date, plane] = jnp.where(upper, own[date, plane, rows - HALO :], own[date, plane, :HALO])


def prepare(own, pieces):
    dates_dev, planes, rows, cols = own.shape
    vmem = pl.BlockSpec(memory_space=pltpu.VMEM)
    shapes = [jax.ShapeDtypeStruct((dates_dev, planes, HALO, cols), own.dtype)]
    shapes += [jax.ShapeDtypeStruct((1, len(p) * rows, width), own.dtype) for p, width in pieces]
    return pl.pallas_call(
        functools.partial(prepare_kernel, [p for p, _ in pieces]),
        out_shape=shapes,
        in_specs=[vmem],
        out_specs=[vmem] * len(shapes),
        name="prepare",
        compiler_params=pltpu.CompilerParams(vmem_limit_bytes=16 << 20),
    )(own)


def table_kernel(total_dates, dates_dev, partners, counts, windows, table, partners_at, counts_at, windows_at, sems):
    pairs = ((partners, partners_at), (counts, counts_at), (windows, windows_at))
    copies = [pltpu.make_async_copy(source, target, sems.at[k]) for k, (source, target) in enumerate(pairs)]
    for copy in copies:
        copy.start()
    for copy in copies:
        copy.wait()
    first_date = lax.axis_index("date") * dates_dev
    row, column = (lax.broadcasted_iota(jnp.int32, table.shape, k) for k in range(2))
    found = jnp.full(table.shape, -1, jnp.int32)
    for date in range(dates_dev):
        for slot in range(partners.shape[1]):
            ahead = partners_at[date, slot] - first_date
            ahead = jnp.where(ahead < 0, ahead + total_dates, ahead)
            code = jnp.where(slot < counts_at[date], slot * CODE + windows_at[date, slot], -1)
            here = jnp.logical_and(row == ahead, column == date)
            found = jnp.maximum(found, jnp.where(here, code, -1))
    table[...] = found


def table_of(partners, counts, windows, total_dates, reached):
    anywhere = pl.BlockSpec(memory_space=pl.ANY)
    return pl.pallas_call(
        functools.partial(table_kernel, total_dates, partners.shape[0]),
        out_shape=jax.ShapeDtypeStruct((reached, partners.shape[0]), jnp.int32),
        in_specs=[anywhere] * 3,
        out_specs=pl.BlockSpec(memory_space=pltpu.VMEM),
        scratch_shapes=[pltpu.SMEM(x.shape, x.dtype) for x in (partners, counts, windows)]
        + [pltpu.SemaphoreType.DMA((3,))],
        name="table",
        compiler_params=pltpu.CompilerParams(vmem_limit_bytes=1 << 20),
    )(partners, counts, windows)


def attach_kernel(pieces, own, own_edge, part):
    dates_dev, planes, rows, _ = own.shape
    gather_rows(part, own, pieces)
    for date in range(dates_dev):
        for plane in range(planes):
            start = len(pieces) * rows + (planes * date + plane) * HALO
            part[0, start : start + HALO] = own_edge[date, plane]


def attach(own, own_edge, pieces):
    dates_dev, planes, rows, cols = own.shape
    vmem = pl.BlockSpec(memory_space=pltpu.VMEM)
    return pl.pallas_call(
        functools.partial(attach_kernel, pieces),
        out_shape=jax.ShapeDtypeStruct((1, len(pieces) * rows + dates_dev * planes * HALO, cols), own.dtype),
        in_specs=[vmem] * 2,
        out_specs=vmem,
        name="attach",
        compiler_params=pltpu.CompilerParams(vmem_limit_bytes=16 << 20),
    )(own, own_edge)


def relayed(own, loop_size, edge_move):
    rows = own.shape[2]
    by_two = [((i + 2) % loop_size, i) for i in range(loop_size)]
    by_one = [((i + 1) % loop_size, i) for i in range(loop_size)]
    within = [(i + 1 - 2 * (i % 2), i) for i in range(loop_size)]
    is_odd = lax.rem(lax.axis_index("date"), 2) == 1
    cols = own.shape[3]
    edge, first, far_part = prepare(own, ((((0, 0, 0), (0, 1, 0)), cols), (((1, 0, 0), (1, 1, 0)), cols)))
    own_edge = edge_move(edge, 0)
    near_part = attach(own, own_edge, ((1, 0, 0), (1, 1, 0)))
    far_first = lax.ppermute(first, "date", by_two)
    near_second = lax.ppermute(near_part, "date", by_one)
    far_edge = edge_move(edge, 2)
    far_second = lax.ppermute(far_part, "date", by_two)
    chosen = jnp.where(is_odd, first, far_first)
    near_first = lax.ppermute(chosen, "date", within)

    def whole_edges(date):
        return lambda stripe: ((0, 0, 0), (0, rows, 0), (1, date, 0), (1, date, 1))

    return own_edge, [
        ((4,), [far_first, far_edge], whole_edges(0), None),
        ((3,), [near_second], lambda stripe: ((0, 0, 0), (0, rows, 0), (0, 2 * rows + 2 * HALO, 0), (0, 2 * rows + 3 * HALO, 0)), None),
        ((2,), [near_first, near_second], lambda stripe: ((0, 0, 0), (0, rows, 0), (1, 2 * rows, 0), (1, 2 * rows + HALO, 0)), None),
        ((5,), [far_second, far_edge], whole_edges(1), None),
    ]


def whole(slc_stack, partners, counts, windows):
    dates_dev, _, _, _ = slc_stack.shape
    per_date = partners.shape[1]
    loop_size = lax.axis_size("date")
    strips = lax.axis_size("row")
    assert strips == 2
    reach = loop_size // 4
    total_dates = dates_dev * loop_size
    reached = (reach + 1) * dates_dev
    tables = (table_of(partners, counts, windows, total_dates, reached), band_table())

    def edge_move(edge, distance):
        pairs = [
            (((i + distance) % loop_size) * strips + (1 - r), i * strips + r) for i in range(loop_size) for r in range(strips)
        ]
        return lax.ppermute(edge, ("date", "row"), pairs)

    if reach == 2 and dates_dev == 2:
        own_edge, arrivals = relayed(slc_stack, loop_size, edge_move)
    else:
        (edge,) = prepare(slc_stack, ())
        own_edge, arrivals = edge_move(edge, 0), []
        for distance in range(1, reach + 1):
            block = lax.ppermute(slc_stack, "date", [((i + distance) % loop_size, i) for i in range(loop_size)])
            rows_of = tuple(range(distance * dates_dev, (distance + 1) * dates_dev))
            arrivals.append((rows_of, [block, edge_move(edge, distance)], None, None))
    places = [tuple(range(dates_dev))]
    own = (tables, slc_stack, own_edge)
    result, own_box = stage("first", places[0], *own, [slc_stack, own_edge], None, None)
    results = [result]
    for number, (rows_of, *block) in enumerate(arrivals):
        left = len(arrivals) - number
        if left > 2:
            results.append(stage("middle", rows_of, *own, *block, own_box))
            places.append(rows_of)
        elif left == 2:
            known = {"places": tuple(places), "final_rows": arrivals[-1][0], "slots": per_date}
            out = stage("gather", rows_of, *own, *block, own_box, *results, **known)
        else:
            out = stage("final", rows_of, *own, *block, own_box, out, slots=per_date)
    return out


def solution(mesh):
    in_specs = (
        P("date", None, ("tiles", "row"), None),
        P("date", None),
        P("date"),
        P("date", None),
    )
    out_specs = P("date", None, ("tiles", "row"), None)
    return jax.shard_map(whole, mesh=mesh, in_specs=in_specs, out_specs=out_specs, check_vma=False)
```

```python
import functools

import jax
import jax.numpy as jnp
from jax import lax
from jax.experimental import pallas as pl
from jax.experimental.pallas import tpu as pltpu
from jax.sharding import PartitionSpec as P


NARROW = 3
WIDE = 5
HALO = 2
LANES = 128
BLOCK = 2 * LANES
TOP = 8
SMALLEST = 1.1754944e-38
CODE = 8


def band_table():
    shape = (WIDE - NARROW + 1, 2 * BLOCK, BLOCK)
    width = lax.broadcasted_iota(jnp.int32, shape, 0) + NARROW
    off = lax.broadcasted_iota(jnp.int32, shape, 1) - LANES - lax.broadcasted_iota(jnp.int32, shape, 2)
    return jnp.where(jnp.abs(off) <= width, 1.0, 0.0).astype(jnp.bfloat16)


def stage_kernel(role, rows_of, layout, span, places, final_rows, blocks, *refs):
    table, bands, own, own_edge, *refs = refs
    other, refs = refs[:blocks], refs[blocks:]
    dates_dev, _, rows, cols = own.shape
    here = len(rows_of)
    stripes = cols // LANES
    wide = BLOCK // LANES
    near_stripes = range(max(0, span[0] * wide - 1), min(stripes, span[1] * wide + 1))
    upper = lax.axis_index("row") == 0
    if role == "first":
        results, own_box, products, split, other_power = refs
    elif role == "middle":
        own_box, results, products, split, other_power = refs
    elif role == "gather":
        own_box, *refs = refs
        earlier, refs = refs[: len(places)], refs[len(places) :]
        out, products, split, other_power, results, sems, zeros, zero_sems = refs
    else:
        own_box, *refs = refs
        earlier, refs = refs[: len(places)], refs[len(places) :]
        _, out, products, split, other_power, results, sems = refs
    codes = table[...]

    def pad(ref, at):
        if span[0] == 0:
            ref[at, :, 0:LANES] = jnp.zeros((ref.shape[1], LANES), jnp.bfloat16)
        if span[1] * BLOCK == cols:
            ref[at, :, LANES + cols :] = jnp.zeros((ref.shape[1], LANES), jnp.bfloat16)

    def over_rows(ref, at, stripe, k, main, edge):
        products[k, TOP : TOP + rows, :] = main
        products[k, TOP - HALO : TOP, :] = jnp.where(upper, 0.0, edge)
        products[k, TOP + rows : TOP + rows + HALO, :] = jnp.where(upper, edge, 0.0)
        total = products[k, TOP - HALO : TOP - HALO + rows, :]
        for shift in range(1, 2 * HALO + 1):
            total = total + products[k, TOP - HALO + shift : TOP - HALO + shift + rows, :]
        high = total.astype(jnp.bfloat16)
        low = (total - high.astype(jnp.float32)).astype(jnp.bfloat16)
        into = slice(LANES + stripe * LANES, LANES + (stripe + 1) * LANES)
        ref[at, 2 * k * rows : (2 * k + 1) * rows, into] = high
        ref[at, (2 * k + 1) * rows : (2 * k + 2) * rows, into] = low

    def stripe_of(ref, at, stripe):
        columns = slice(stripe * LANES, (stripe + 1) * LANES)
        return tuple(ref[at, plane, :, columns].astype(jnp.float32) for plane in range(2))

    def own_stripe(date, stripe):
        return *stripe_of(own, date, stripe), *stripe_of(own_edge, date, stripe)

    def other_stripe(t, stripe):
        if layout is None:
            return *stripe_of(other[0], t, stripe), *stripe_of(other[1], t, stripe)
        found = []
        for (k, start, base), size in zip(layout(stripe), (rows, rows, HALO, HALO)):
            if len(other[k].shape) == 4:
                found.append(other[k][start, base, :, stripe * LANES : (stripe + 1) * LANES].astype(jnp.float32))
                continue
            columns = slice((stripe - base) * LANES, (stripe - base + 1) * LANES)
            found.append(other[k][0, start : start + size, columns].astype(jnp.float32))
        return found

    def fill_power(ref, at, source, source_at):
        pad(ref, at)
        for stripe in near_stripes:
            re, im, edge_re, edge_im = source(source_at, stripe)
            over_rows(ref, at, stripe, 0, re * re + im * im, edge_re * edge_re + edge_im * edge_im)

    def over_columns(parts, width):
        box = jnp.dot(jnp.concatenate(parts, axis=0), bands[width], preferred_element_type=jnp.float32)
        return [box[k : k + rows] + box[k + rows : k + 2 * rows] for k in range(0, box.shape[0], 2 * rows)]

    def fill_box(power, date):
        for width in range(bands.shape[0]):
            for j in range(*span):
                (total,) = over_columns([power[date, :, j * BLOCK : (j + 2) * BLOCK]], width)
                own_box[date, width, :, j * BLOCK : (j + 1) * BLOCK] = total

    def pair(t, date, code):
        width = code % CODE - NARROW
        for stripe in near_stripes:
            u_re, u_im, ue_re, ue_im = own_stripe(date, stripe)
            v_re, v_im, ve_re, ve_im = other_stripe(t, stripe)
            over_rows(split, 0, stripe, 0, u_re * v_re + u_im * v_im, ue_re * ve_re + ue_im * ve_im)
            over_rows(split, 0, stripe, 1, u_im * v_re - u_re * v_im, ue_im * ve_re - ue_re * ve_im)
        for j in range(*span):
            at = slice(j * BLOCK, (j + 2) * BLOCK)
            re, im, power = over_columns([split[0, :, at], other_power[t, :, at]], width)
            square = re * re + im * im
            magnitude = square * lax.rsqrt(jnp.maximum(square, SMALLEST))
            value = magnitude * lax.rsqrt(own_box[date, width, :, j * BLOCK : (j + 1) * BLOCK] * power)
            results[t * dates_dev + date, :, j * BLOCK : (j + 1) * BLOCK] = value.astype(jnp.bfloat16)

    def copy_of(ref, at, date, slot, number):
        source, target = ref.at[at], out.at[date, slot]
        if ref is results and span != (0, cols // BLOCK):
            columns = slice(span[0] * BLOCK, span[1] * BLOCK)
            source, target = ref.at[at, :, columns], out.at[date, slot, :, columns]
        return pltpu.make_async_copy(source, target, sems.at[number + at])

    def copies_of(ref, rows_at, number):
        found = []
        for t, row in enumerate(rows_at):
            for date in range(dates_dev):
                code, at = codes[row, date], t * dates_dev + date
                found.append((code >= 0, copy_of(ref, at, date, jnp.maximum(code, 0) // CODE, number)))
        return found

    def zero_copies():
        found = []
        for date in range(dates_dev):
            held = [codes[row, date] // CODE for rows_at in (*places, rows_of, *final_rows) for row in rows_at]
            for slot in range(out.shape[1]):
                empty = functools.reduce(jnp.logical_and, [code != slot for code in held])
                at = date * out.shape[1] + slot
                found.append((empty, pltpu.make_async_copy(zeros, out.at[date, slot], zero_sems.at[at])))
        return found

    def each(items, action):
        for condition, copy in items:

            @pl.when(condition)
            def _(copy=copy):
                getattr(copy, action)()

    pending, own_copies = [], []
    if role in ("gather", "final"):
        number = here * dates_dev
        for ref, rows_at in zip(earlier, places):
            pending += copies_of(ref, rows_at, number)
            number += len(rows_at) * dates_dev
        if role == "gather":
            zeros[...] = jnp.zeros_like(zeros)
            pending += zero_copies()
        each(pending, "start")
        own_copies = copies_of(results, rows_of, 0)
    if role == "first":
        for date in range(dates_dev):
            fill_power(other_power, date, own_stripe, date)
            fill_box(other_power, date)
    for t, row in enumerate(rows_of):
        found = [codes[row, date] for date in range(dates_dev)]

        @pl.when(functools.reduce(jnp.maximum, found) >= 0)
        def _(t=t, found=found):
            pad(split, 0)
            if role != "first":
                fill_power(other_power, t, other_stripe, t)

            def body(date, carry):
                code = found[0]
                for k in range(1, dates_dev):
                    code = jnp.where(date == k, found[k], code)

                @pl.when(code >= 0)
                def _():
                    pair(t, date, code)
                    if own_copies:
                        copy_of(results, t * dates_dev + date, date, code // CODE, 0).start()

                return carry

            lax.fori_loop(0, dates_dev, body, 0)

    each(pending + own_copies, "wait")


def stage(role, rows_of, tables, own, own_edge, other, layout, span, *state, places=(), final_rows=(), slots=None):
    dates_dev, _, rows, cols = own.shape
    here = len(rows_of)
    vmem, anywhere = pl.BlockSpec(memory_space=pltpu.VMEM), pl.BlockSpec(memory_space=pl.ANY)
    padded = cols + BLOCK
    span = span or (0, cols // BLOCK)
    results = (here * dates_dev, rows, cols)
    scratch = [pltpu.VMEM((2, rows + 2 * TOP, LANES), jnp.float32), pltpu.VMEM((1, 4 * rows, padded), jnp.bfloat16)]
    scratch.append(pltpu.VMEM((here, 2 * rows, padded), jnp.bfloat16))
    out_shape, out_specs = jax.ShapeDtypeStruct(results, jnp.bfloat16), vmem
    if role == "first":
        out_shape = (out_shape, jax.ShapeDtypeStruct((dates_dev, WIDE - NARROW + 1, rows, cols), jnp.float32))
        out_specs = (vmem, vmem)
    args = [*tables, own, own_edge, *other, *state]
    in_specs = [vmem] * len(args)
    aliases = {}
    if role in ("gather", "final"):
        out_shape, out_specs = jax.ShapeDtypeStruct((dates_dev, slots, rows, cols), jnp.bfloat16), anywhere
        count = here + sum(len(p) for p in places)
        scratch += [pltpu.VMEM(results, jnp.bfloat16), pltpu.SemaphoreType.DMA((count * dates_dev,))]
    if role == "gather":
        scratch += [pltpu.VMEM((rows, cols), jnp.bfloat16), pltpu.SemaphoreType.DMA((dates_dev * slots,))]
    if role == "final":
        in_specs[-1] = anywhere
        aliases = {len(args) - 1: 0}
    return pl.pallas_call(
        functools.partial(stage_kernel, role, rows_of, layout, span, places, final_rows, len(other)),
        out_shape=out_shape,
        in_specs=in_specs,
        out_specs=out_specs,
        scratch_shapes=scratch,
        input_output_aliases=aliases,
        compiler_params=pltpu.CompilerParams(vmem_limit_bytes=16 << 20),
        cost_estimate=pl.CostEstimate(flops=1 << 30, bytes_accessed=1 << 22, transcendentals=0),
    )(*args)


def gather_rows(part, own, pieces):
    rows = own.shape[2]
    for k, (date, plane, column) in enumerate(pieces):
        part[0, k * rows : (k + 1) * rows] = own[date, plane, :, column : column + part.shape[2]]


def prepare_kernel(pieces, own, edge, *parts):
    dates_dev, planes, rows, _ = own.shape
    upper = lax.axis_index("row") == 0
    for part, pieces_of in zip(parts, pieces):
        gather_rows(part, own, pieces_of)
    for date in range(dates_dev):
        for plane in range(planes):
            edge[date, plane] = jnp.where(upper, own[date, plane, rows - HALO :], own[date, plane, :HALO])


def prepare(own, pieces):
    dates_dev, planes, rows, cols = own.shape
    vmem = pl.BlockSpec(memory_space=pltpu.VMEM)
    shapes = [jax.ShapeDtypeStruct((dates_dev, planes, HALO, cols), own.dtype)]
    shapes += [jax.ShapeDtypeStruct((1, len(p) * rows, width), own.dtype) for p, width in pieces]
    return pl.pallas_call(
        functools.partial(prepare_kernel, [p for p, _ in pieces]),
        out_shape=shapes,
        in_specs=[vmem],
        out_specs=[vmem] * len(shapes),
        name="prepare",
        compiler_params=pltpu.CompilerParams(vmem_limit_bytes=16 << 20),
    )(own)


def table_kernel(total_dates, dates_dev, partners, counts, windows, table, partners_at, counts_at, windows_at, sems):
    pairs = ((partners, partners_at), (counts, counts_at), (windows, windows_at))
    copies = [pltpu.make_async_copy(source, target, sems.at[k]) for k, (source, target) in enumerate(pairs)]
    for copy in copies:
        copy.start()
    for copy in copies:
        copy.wait()
    first_date = lax.axis_index("date") * dates_dev
    row, column = (lax.broadcasted_iota(jnp.int32, table.shape, k) for k in range(2))
    found = jnp.full(table.shape, -1, jnp.int32)
    for date in range(dates_dev):
        for slot in range(partners.shape[1]):
            ahead = partners_at[date, slot] - first_date
            ahead = jnp.where(ahead < 0, ahead + total_dates, ahead)
            code = jnp.where(slot < counts_at[date], slot * CODE + windows_at[date, slot], -1)
            here = jnp.logical_and(row == ahead, column == date)
            found = jnp.maximum(found, jnp.where(here, code, -1))
    table[...] = found


def table_of(partners, counts, windows, total_dates, reached):
    anywhere = pl.BlockSpec(memory_space=pl.ANY)
    return pl.pallas_call(
        functools.partial(table_kernel, total_dates, partners.shape[0]),
        out_shape=jax.ShapeDtypeStruct((reached, partners.shape[0]), jnp.int32),
        in_specs=[anywhere] * 3,
        out_specs=pl.BlockSpec(memory_space=pltpu.VMEM),
        scratch_shapes=[pltpu.SMEM(x.shape, x.dtype) for x in (partners, counts, windows)]
        + [pltpu.SemaphoreType.DMA((3,))],
        name="table",
        compiler_params=pltpu.CompilerParams(vmem_limit_bytes=1 << 20),
    )(partners, counts, windows)


def attach_kernel(pieces, own, own_edge, part):
    dates_dev, planes, rows, _ = own.shape
    gather_rows(part, own, pieces)
    for date in range(dates_dev):
        for plane in range(planes):
            start = len(pieces) * rows + (planes * date + plane) * HALO
            part[0, start : start + HALO] = own_edge[date, plane]


def attach(own, own_edge, pieces):
    dates_dev, planes, rows, cols = own.shape
    vmem = pl.BlockSpec(memory_space=pltpu.VMEM)
    return pl.pallas_call(
        functools.partial(attach_kernel, pieces),
        out_shape=jax.ShapeDtypeStruct((1, len(pieces) * rows + dates_dev * planes * HALO, cols), own.dtype),
        in_specs=[vmem] * 2,
        out_specs=vmem,
        name="attach",
        compiler_params=pltpu.CompilerParams(vmem_limit_bytes=16 << 20),
    )(own, own_edge)


def relayed(own, loop_size, edge_move):
    rows = own.shape[2]
    by_two = [((i + 2) % loop_size, i) for i in range(loop_size)]
    by_one = [((i + 1) % loop_size, i) for i in range(loop_size)]
    within = [(i + 1 - 2 * (i % 2), i) for i in range(loop_size)]
    is_odd = lax.rem(lax.axis_index("date"), 2) == 1
    cols = own.shape[3]
    edge, first, far_part = prepare(own, ((((0, 0, 0), (0, 1, 0)), cols), (((1, 0, 0), (1, 1, 0)), cols)))
    own_edge = edge_move(edge, 0)
    near_part = attach(own, own_edge, ((1, 0, 0), (1, 1, 0)))
    far_first = lax.ppermute(first, "date", by_two)
    near_second = lax.ppermute(near_part, "date", by_one)
    far_edge = edge_move(edge, 2)
    far_second = lax.ppermute(far_part, "date", by_two)
    chosen = jnp.where(is_odd, first, far_first)
    near_first = lax.ppermute(chosen, "date", within)

    def whole_edges(date):
        return lambda stripe: ((0, 0, 0), (0, rows, 0), (1, date, 0), (1, date, 1))

    return own_edge, [
        ((4,), [far_first, far_edge], whole_edges(0), None),
        ((3,), [near_second], lambda stripe: ((0, 0, 0), (0, rows, 0), (0, 2 * rows + 2 * HALO, 0), (0, 2 * rows + 3 * HALO, 0)), None),
        ((2,), [near_first, near_second], lambda stripe: ((0, 0, 0), (0, rows, 0), (1, 2 * rows, 0), (1, 2 * rows + HALO, 0)), None),
        ((5,), [far_second, far_edge], whole_edges(1), None),
    ]


def whole(slc_stack, partners, counts, windows):
    dates_dev, _, _, _ = slc_stack.shape
    per_date = partners.shape[1]
    loop_size = lax.axis_size("date")
    strips = lax.axis_size("row")
    assert strips == 2
    reach = loop_size // 4
    total_dates = dates_dev * loop_size
    reached = (reach + 1) * dates_dev
    tables = (table_of(partners, counts, windows, total_dates, reached), band_table())

    def edge_move(edge, distance):
        pairs = [
            (((i + distance) % loop_size) * strips + (1 - r), i * strips + r) for i in range(loop_size) for r in range(strips)
        ]
        return lax.ppermute(edge, ("date", "row"), pairs)

    if reach == 2 and dates_dev == 2:
        own_edge, arrivals = relayed(slc_stack, loop_size, edge_move)
    else:
        (edge,) = prepare(slc_stack, ())
        own_edge, arrivals = edge_move(edge, 0), []
        for distance in range(1, reach + 1):
            block = lax.ppermute(slc_stack, "date", [((i + distance) % loop_size, i) for i in range(loop_size)])
            rows_of = tuple(range(distance * dates_dev, (distance + 1) * dates_dev))
            arrivals.append((rows_of, [block, edge_move(edge, distance)], None, None))
    places = [tuple(range(dates_dev))]
    own = (tables, slc_stack, own_edge)
    result, own_box = stage("first", places[0], *own, [slc_stack, own_edge], None, None)
    results = [result]
    for number, (rows_of, *block) in enumerate(arrivals):
        left = len(arrivals) - number
        if left == 3:
            known = {"places": tuple(places), "final_rows": tuple(a[0] for a in arrivals[-2:]), "slots": per_date}
            out = stage("gather", rows_of, *own, *block, own_box, *results, **known)
            places, results = [], []
        elif left == 1:
            out = stage("final", rows_of, *own, *block, own_box, *results, out, places=tuple(places), slots=per_date)
        else:
            results.append(stage("middle", rows_of, *own, *block, own_box))
            places.append(rows_of)
    return out


def solution(mesh):
    in_specs = (
        P("date", None, ("tiles", "row"), None),
        P("date", None),
        P("date"),
        P("date", None),
    )
    out_specs = P("date", None, ("tiles", "row"), None)
    return jax.shard_map(whole, mesh=mesh, in_specs=in_specs, out_specs=out_specs, check_vma=False)
```

```python
import functools

import jax
import jax.numpy as jnp
from jax import lax
from jax.experimental import pallas as pl
from jax.experimental.pallas import tpu as pltpu
from jax.sharding import PartitionSpec as P


NARROW = 3
WIDE = 5
HALO = 2
LANES = 128
BLOCK = 2 * LANES
TOP = 8
SMALLEST = 1.1754944e-38
CODE = 8


def band_table():
    shape = (WIDE - NARROW + 1, 2 * BLOCK, BLOCK)
    width = lax.broadcasted_iota(jnp.int32, shape, 0) + NARROW
    off = lax.broadcasted_iota(jnp.int32, shape, 1) - LANES - lax.broadcasted_iota(jnp.int32, shape, 2)
    return jnp.where(jnp.abs(off) <= width, 1.0, 0.0).astype(jnp.bfloat16)


def stage_kernel(role, rows_of, layout, span, places, final_rows, blocks, *refs):
    table, bands, own, own_edge, *refs = refs
    other, refs = refs[:blocks], refs[blocks:]
    dates_dev, _, rows, cols = own.shape
    here = len(rows_of)
    stripes = cols // LANES
    wide = BLOCK // LANES
    near_stripes = range(max(0, span[0] * wide - 1), min(stripes, span[1] * wide + 1))
    upper = lax.axis_index("row") == 0
    if role == "first":
        results, own_box, products, split, other_power = refs
    elif role == "middle":
        own_box, results, products, split, other_power = refs
    elif role == "gather":
        own_box, *refs = refs
        earlier, refs = refs[: len(places)], refs[len(places) :]
        out, products, split, other_power, results, sems, zeros, zero_sems = refs
    else:
        own_box, *refs = refs
        earlier, refs = refs[: len(places)], refs[len(places) :]
        _, out, products, split, other_power, results, sems = refs
    codes = table[...]

    def pad(ref, at):
        if span[0] == 0:
            ref[at, :, 0:LANES] = jnp.zeros((ref.shape[1], LANES), jnp.bfloat16)
        if span[1] * BLOCK == cols:
            ref[at, :, LANES + cols :] = jnp.zeros((ref.shape[1], LANES), jnp.bfloat16)

    def over_rows(ref, at, stripe, k, main, edge):
        products[k, TOP : TOP + rows, :] = main
        products[k, TOP - HALO : TOP, :] = jnp.where(upper, 0.0, edge)
        products[k, TOP + rows : TOP + rows + HALO, :] = jnp.where(upper, edge, 0.0)
        total = products[k, TOP - HALO : TOP - HALO + rows, :]
        for shift in range(1, 2 * HALO + 1):
            total = total + products[k, TOP - HALO + shift : TOP - HALO + shift + rows, :]
        high = total.astype(jnp.bfloat16)
        low = (total - high.astype(jnp.float32)).astype(jnp.bfloat16)
        into = slice(LANES + stripe * LANES, LANES + (stripe + 1) * LANES)
        ref[at, 2 * k * rows : (2 * k + 1) * rows, into] = high
        ref[at, (2 * k + 1) * rows : (2 * k + 2) * rows, into] = low

    def stripe_of(ref, at, stripe):
        columns = slice(stripe * LANES, (stripe + 1) * LANES)
        return tuple(ref[at, plane, :, columns].astype(jnp.float32) for plane in range(2))

    def own_stripe(date, stripe):
        return *stripe_of(own, date, stripe), *stripe_of(own_edge, date, stripe)

    def other_stripe(t, stripe):
        if layout is None:
            return *stripe_of(other[0], t, stripe), *stripe_of(other[1], t, stripe)
        found = []
        for (k, start, base), size in zip(layout(stripe), (rows, rows, HALO, HALO)):
            columns = slice((stripe - base) * LANES, (stripe - base + 1) * LANES)
            found.append(other[k][0, start : start + size, columns].astype(jnp.float32))
        return found

    def fill_power(ref, at, source, source_at):
        pad(ref, at)
        for stripe in near_stripes:
            re, im, edge_re, edge_im = source(source_at, stripe)
            over_rows(ref, at, stripe, 0, re * re + im * im, edge_re * edge_re + edge_im * edge_im)

    def over_columns(parts, width):
        box = jnp.dot(jnp.concatenate(parts, axis=0), bands[width], preferred_element_type=jnp.float32)
        return [box[k : k + rows] + box[k + rows : k + 2 * rows] for k in range(0, box.shape[0], 2 * rows)]

    def fill_box(power, date):
        for width in range(bands.shape[0]):
            for j in range(*span):
                (total,) = over_columns([power[date, :, j * BLOCK : (j + 2) * BLOCK]], width)
                own_box[date, width, :, j * BLOCK : (j + 1) * BLOCK] = total

    def pair(t, date, code):
        width = code % CODE - NARROW
        for stripe in near_stripes:
            u_re, u_im, ue_re, ue_im = own_stripe(date, stripe)
            v_re, v_im, ve_re, ve_im = other_stripe(t, stripe)
            over_rows(split, 0, stripe, 0, u_re * v_re + u_im * v_im, ue_re * ve_re + ue_im * ve_im)
            over_rows(split, 0, stripe, 1, u_im * v_re - u_re * v_im, ue_im * ve_re - ue_re * ve_im)
        for j in range(*span):
            at = slice(j * BLOCK, (j + 2) * BLOCK)
            re, im, power = over_columns([split[0, :, at], other_power[t, :, at]], width)
            square = re * re + im * im
            magnitude = square * lax.rsqrt(jnp.maximum(square, SMALLEST))
            value = magnitude * lax.rsqrt(own_box[date, width, :, j * BLOCK : (j + 1) * BLOCK] * power)
            results[t * dates_dev + date, :, j * BLOCK : (j + 1) * BLOCK] = value.astype(jnp.bfloat16)

    def copy_of(ref, at, date, slot, number):
        source, target = ref.at[at], out.at[date, slot]
        if ref is results and span != (0, cols // BLOCK):
            columns = slice(span[0] * BLOCK, span[1] * BLOCK)
            source, target = ref.at[at, :, columns], out.at[date, slot, :, columns]
        return pltpu.make_async_copy(source, target, sems.at[number + at])

    def copies_of(ref, rows_at, number):
        found = []
        for t, row in enumerate(rows_at):
            for date in range(dates_dev):
                code, at = codes[row, date], t * dates_dev + date
                found.append((code >= 0, copy_of(ref, at, date, jnp.maximum(code, 0) // CODE, number)))
        return found

    def zero_copies():
        found = []
        for date in range(dates_dev):
            held = [codes[row, date] // CODE for rows_at in (*places, rows_of, *final_rows) for row in rows_at]
            for slot in range(out.shape[1]):
                empty = functools.reduce(jnp.logical_and, [code != slot for code in held])
                at = date * out.shape[1] + slot
                found.append((empty, pltpu.make_async_copy(zeros, out.at[date, slot], zero_sems.at[at])))
        return found

    def each(items, action):
        for condition, copy in items:

            @pl.when(condition)
            def _(copy=copy):
                getattr(copy, action)()

    pending, own_copies = [], []
    if role in ("gather", "final"):
        number = here * dates_dev
        for ref, rows_at in zip(earlier, places):
            pending += copies_of(ref, rows_at, number)
            number += len(rows_at) * dates_dev
        if role == "gather":
            zeros[...] = jnp.zeros_like(zeros)
            pending += zero_copies()
        each(pending, "start")
        own_copies = copies_of(results, rows_of, 0)
    if role == "first":
        for date in range(dates_dev):
            fill_power(other_power, date, own_stripe, date)
            fill_box(other_power, date)
    for t, row in enumerate(rows_of):
        found = [codes[row, date] for date in range(dates_dev)]

        @pl.when(functools.reduce(jnp.maximum, found) >= 0)
        def _(t=t, found=found):
            pad(split, 0)
            if role != "first":
                fill_power(other_power, t, other_stripe, t)

            def body(date, carry):
                code = found[0]
                for k in range(1, dates_dev):
                    code = jnp.where(date == k, found[k], code)

                @pl.when(code >= 0)
                def _():
                    pair(t, date, code)
                    if own_copies:
                        copy_of(results, t * dates_dev + date, date, code // CODE, 0).start()

                return carry

            lax.fori_loop(0, dates_dev, body, 0)

    each(pending + own_copies, "wait")


def stage(role, rows_of, tables, own, own_edge, other, layout, span, *state, places=(), final_rows=(), slots=None):
    dates_dev, _, rows, cols = own.shape
    here = len(rows_of)
    vmem, anywhere = pl.BlockSpec(memory_space=pltpu.VMEM), pl.BlockSpec(memory_space=pl.ANY)
    padded = cols + BLOCK
    span = span or (0, cols // BLOCK)
    results = (here * dates_dev, rows, cols)
    scratch = [pltpu.VMEM((2, rows + 2 * TOP, LANES), jnp.float32), pltpu.VMEM((1, 4 * rows, padded), jnp.bfloat16)]
    scratch.append(pltpu.VMEM((here, 2 * rows, padded), jnp.bfloat16))
    out_shape, out_specs = jax.ShapeDtypeStruct(results, jnp.bfloat16), vmem
    if role == "first":
        out_shape = (out_shape, jax.ShapeDtypeStruct((dates_dev, WIDE - NARROW + 1, rows, cols), jnp.float32))
        out_specs = (vmem, vmem)
    args = [*tables, own, own_edge, *other, *state]
    in_specs = [vmem] * len(args)
    aliases = {}
    if role in ("gather", "final"):
        out_shape, out_specs = jax.ShapeDtypeStruct((dates_dev, slots, rows, cols), jnp.bfloat16), anywhere
        count = here + sum(len(p) for p in places)
        scratch += [pltpu.VMEM(results, jnp.bfloat16), pltpu.SemaphoreType.DMA((count * dates_dev,))]
    if role == "gather":
        scratch += [pltpu.VMEM((rows, cols), jnp.bfloat16), pltpu.SemaphoreType.DMA((dates_dev * slots,))]
    if role == "final":
        in_specs[-1] = anywhere
        aliases = {len(args) - 1: 0}
    return pl.pallas_call(
        functools.partial(stage_kernel, role, rows_of, layout, span, places, final_rows, len(other)),
        out_shape=out_shape,
        in_specs=in_specs,
        out_specs=out_specs,
        scratch_shapes=scratch,
        input_output_aliases=aliases,
        compiler_params=pltpu.CompilerParams(vmem_limit_bytes=16 << 20),
        cost_estimate=pl.CostEstimate(flops=1 << 30, bytes_accessed=1 << 22, transcendentals=0),
    )(*args)


def gather_rows(part, own, pieces):
    rows = own.shape[2]
    for k, (date, plane, column) in enumerate(pieces):
        part[0, k * rows : (k + 1) * rows] = own[date, plane, :, column : column + part.shape[2]]


def prepare_kernel(pieces, own, edge, *parts):
    dates_dev, planes, rows, _ = own.shape
    upper = lax.axis_index("row") == 0
    for part, pieces_of in zip(parts, pieces):
        gather_rows(part, own, pieces_of)
    for date in range(dates_dev):
        for plane in range(planes):
            edge[date, plane] = jnp.where(upper, own[date, plane, rows - HALO :], own[date, plane, :HALO])


def prepare(own, pieces):
    dates_dev, planes, rows, cols = own.shape
    vmem = pl.BlockSpec(memory_space=pltpu.VMEM)
    shapes = [jax.ShapeDtypeStruct((dates_dev, planes, HALO, cols), own.dtype)]
    shapes += [jax.ShapeDtypeStruct((1, len(p) * rows, width), own.dtype) for p, width in pieces]
    return pl.pallas_call(
        functools.partial(prepare_kernel, [p for p, _ in pieces]),
        out_shape=shapes,
        in_specs=[vmem],
        out_specs=[vmem] * len(shapes),
        name="prepare",
        compiler_params=pltpu.CompilerParams(vmem_limit_bytes=16 << 20),
    )(own)


def table_kernel(total_dates, dates_dev, partners, counts, windows, table, partners_at, counts_at, windows_at, sems):
    pairs = ((partners, partners_at), (counts, counts_at), (windows, windows_at))
    copies = [pltpu.make_async_copy(source, target, sems.at[k]) for k, (source, target) in enumerate(pairs)]
    for copy in copies:
        copy.start()
    for copy in copies:
        copy.wait()
    first_date = lax.axis_index("date") * dates_dev
    row, column = (lax.broadcasted_iota(jnp.int32, table.shape, k) for k in range(2))
    found = jnp.full(table.shape, -1, jnp.int32)
    for date in range(dates_dev):
        for slot in range(partners.shape[1]):
            ahead = partners_at[date, slot] - first_date
            ahead = jnp.where(ahead < 0, ahead + total_dates, ahead)
            code = jnp.where(slot < counts_at[date], slot * CODE + windows_at[date, slot], -1)
            here = jnp.logical_and(row == ahead, column == date)
            found = jnp.maximum(found, jnp.where(here, code, -1))
    table[...] = found


def table_of(partners, counts, windows, total_dates, reached):
    anywhere = pl.BlockSpec(memory_space=pl.ANY)
    return pl.pallas_call(
        functools.partial(table_kernel, total_dates, partners.shape[0]),
        out_shape=jax.ShapeDtypeStruct((reached, partners.shape[0]), jnp.int32),
        in_specs=[anywhere] * 3,
        out_specs=pl.BlockSpec(memory_space=pltpu.VMEM),
        scratch_shapes=[pltpu.SMEM(x.shape, x.dtype) for x in (partners, counts, windows)]
        + [pltpu.SemaphoreType.DMA((3,))],
        name="table",
        compiler_params=pltpu.CompilerParams(vmem_limit_bytes=1 << 20),
    )(partners, counts, windows)


def attach_kernel(pieces, own, own_edge, part):
    dates_dev, planes, rows, _ = own.shape
    gather_rows(part, own, pieces)
    for date in range(dates_dev):
        for plane in range(planes):
            start = len(pieces) * rows + (planes * date + plane) * HALO
            part[0, start : start + HALO] = own_edge[date, plane]


def attach(own, own_edge, pieces):
    dates_dev, planes, rows, cols = own.shape
    vmem = pl.BlockSpec(memory_space=pltpu.VMEM)
    return pl.pallas_call(
        functools.partial(attach_kernel, pieces),
        out_shape=jax.ShapeDtypeStruct((1, len(pieces) * rows + dates_dev * planes * HALO, cols), own.dtype),
        in_specs=[vmem] * 2,
        out_specs=vmem,
        name="attach",
        compiler_params=pltpu.CompilerParams(vmem_limit_bytes=16 << 20),
    )(own, own_edge)


def relayed(own, loop_size, edge_move):
    rows = own.shape[2]
    by_two = [((i + 2) % loop_size, i) for i in range(loop_size)]
    by_one = [((i + 1) % loop_size, i) for i in range(loop_size)]
    within = [(i + 1 - 2 * (i % 2), i) for i in range(loop_size)]
    is_odd = lax.rem(lax.axis_index("date"), 2) == 1
    cols = own.shape[3]
    edge, first_re, second = prepare(own, ((((0, 0, 0),), cols), (((1, 0, 0), (1, 1, 0)), cols)))
    own_edge = edge_move(edge, 0)
    parts = first_re, attach(own, own_edge, ((0, 1, 0),))
    far = [lax.ppermute(part, "date", by_two) for part in parts]
    near_second = lax.ppermute(attach(own, own_edge, ((1, 0, 0), (1, 1, 0))), "date", by_one)
    far_second = lax.ppermute(second, "date", by_two)
    near = []
    for k, part in enumerate(parts):
        chosen = jnp.where(is_odd, part, far[k])
        near.append(lax.ppermute(chosen, "date", within))

    def of_first(stripe):
        return (0, 0, 0), (1, 0, 0), (1, rows, 0), (1, rows + HALO, 0)

    def of_near_second(stripe):
        return (0, 0, 0), (0, rows, 0), (0, 2 * rows + 2 * HALO, 0), (0, 2 * rows + 3 * HALO, 0)

    def of_far_second(stripe):
        return (0, 0, 0), (0, rows, 0), (1, rows + 2 * HALO, 0), (1, rows + 3 * HALO, 0)

    return own_edge, [
        ((4,), far, of_first, None),
        ((3,), [near_second], of_near_second, None),
        ((2,), near, of_first, None),
        ((5,), [far_second, far[1]], of_far_second, None),
    ]


def whole(slc_stack, partners, counts, windows):
    dates_dev, _, _, _ = slc_stack.shape
    per_date = partners.shape[1]
    loop_size = lax.axis_size("date")
    strips = lax.axis_size("row")
    assert strips == 2
    reach = loop_size // 4
    total_dates = dates_dev * loop_size
    reached = (reach + 1) * dates_dev
    tables = (table_of(partners, counts, windows, total_dates, reached), band_table())

    def edge_move(edge, distance):
        pairs = [
            (((i + distance) % loop_size) * strips + (1 - r), i * strips + r) for i in range(loop_size) for r in range(strips)
        ]
        return lax.ppermute(edge, ("date", "row"), pairs)

    if reach == 2 and dates_dev == 2:
        own_edge, arrivals = relayed(slc_stack, loop_size, edge_move)
    else:
        (edge,) = prepare(slc_stack, ())
        own_edge, arrivals = edge_move(edge, 0), []
        for distance in range(1, reach + 1):
            block = lax.ppermute(slc_stack, "date", [((i + distance) % loop_size, i) for i in range(loop_size)])
            rows_of = tuple(range(distance * dates_dev, (distance + 1) * dates_dev))
            arrivals.append((rows_of, [block, edge_move(edge, distance)], None, None))
    places = [tuple(range(dates_dev))]
    own = (tables, slc_stack, own_edge)
    result, own_box = stage("first", places[0], *own, [slc_stack, own_edge], None, None)
    results = [result]
    for number, (rows_of, *block) in enumerate(arrivals):
        left = len(arrivals) - number
        if left == 3:
            known = {"places": tuple(places), "final_rows": tuple(a[0] for a in arrivals[-2:]), "slots": per_date}
            out = stage("gather", rows_of, *own, *block, own_box, *results, **known)
            places, results = [], []
        elif left == 1:
            out = stage("final", rows_of, *own, *block, own_box, *results, out, places=tuple(places), slots=per_date)
        else:
            results.append(stage("middle", rows_of, *own, *block, own_box))
            places.append(rows_of)
    return out


def solution(mesh):
    in_specs = (
        P("date", None, ("tiles", "row"), None),
        P("date", None),
        P("date"),
        P("date", None),
    )
    out_specs = P("date", None, ("tiles", "row"), None)
    return jax.shard_map(whole, mesh=mesh, in_specs=in_specs, out_specs=out_specs, check_vma=False)
```
